32 devices in a mesh: fsdp: 32 (over z, y, x, core).
Axes of the slice: x: 2, y: 2, z: 4, core: 2. Of those that a mesh axis runs over, the one named last changes fastest.
Arguments:
- inputs: bfloat16 [64, 512, 768], P('fsdp'), may hold values from -6 to 6
- segments: int32 [64, 512], P('fsdp'), may hold values from 0 to 3, never falling along the last dimension, each value on 1 to 256 neighbouring positions
- query_weight: bfloat16 [589824], P('fsdp'), may hold values from -0.21875 to 0.21875
- query_bias: bfloat16 [768], P('fsdp'), may hold values from -3 to 3
- key_weight: bfloat16 [589824], P('fsdp'), may hold values from -0.21875 to 0.21875
- value_weight: bfloat16 [589824], P('fsdp'), may hold values from -0.21875 to 0.21875
- value_bias: bfloat16 [768], P('fsdp'), may hold values from -3 to 3
- output_weight: bfloat16 [589824], P('fsdp'), may hold values from -0.625 to 0.625
- output_bias: bfloat16 [768], P('fsdp'), may hold values from -2 to 2
- attn_gain: bfloat16 [768], P('fsdp'), may hold values from 0.5 to 1.5
- attn_shift: bfloat16 [768], P('fsdp'), may hold values from -2 to 2
- inner_weight: bfloat16 [2359296], P('fsdp'), may hold values from -0.21875 to 0.21875
- inner_bias: bfloat16 [3072], P('fsdp'), may hold values from -3 to 3
- outer_weight: bfloat16 [2359296], P('fsdp'), may hold values from -0.109375 to 0.109375
- outer_bias: bfloat16 [768], P('fsdp'), may hold values from -2 to 2
- ffn_gain: bfloat16 [768], P('fsdp'), may hold values from 0.5 to 1.5
- ffn_shift: bfloat16 [768], P('fsdp'), may hold values from -2 to 2
- cotangent: bfloat16 [64, 512, 768], P('fsdp'), may hold values from -6 to 6
Outputs:
- output: bfloat16 [64, 512, 768], P('fsdp')
- input_grad: bfloat16 [64, 512, 768], P('fsdp')
- query_weight_grad: float32 [589824], P('fsdp')
- query_bias_grad: float32 [768], P('fsdp')
- key_weight_grad: float32 [589824], P('fsdp')
- value_weight_grad: float32 [589824], P('fsdp')
- value_bias_grad: float32 [768], P('fsdp')
- output_weight_grad: float32 [589824], P('fsdp')
- output_bias_grad: float32 [768], P('fsdp')
- attn_gain_grad: float32 [768], P('fsdp')
- attn_shift_grad: float32 [768], P('fsdp')
- inner_weight_grad: float32 [2359296], P('fsdp')
- inner_bias_grad: float32 [3072], P('fsdp')
- outer_weight_grad: float32 [2359296], P('fsdp')
- outer_bias_grad: float32 [768], P('fsdp')
- ffn_gain_grad: float32 [768], P('fsdp')
- ffn_shift_grad: float32 [768], P('fsdp')
The draws below stay inside these ranges and needn't reach their ends.
Inputs may be any that keep to these rules, and one draw needn't show every extreme that they name: `segments`: within each row of 512 tokens the ids never fall; each of the 4 documents holds 1 to 256 tokens, one exactly 256.
All inputs are finite; a program needn't handle non-finite values.
Results may differ from the reference program's by a relative error of at most 0.013.
Values may be sent and summed in bfloat16 or wider, within the bound.
No kernel may reach another device: no remote copies, remote signals or barrier semaphores. Data moves between devices by JAX's collectives and lax.ppermute only.
A program may use at most 192 MiB of HBM per device.

```python
import math
import jax
import jax.numpy as jnp
import numpy as np
from jax import lax

D = 768
H = 12
HD = 64
FF = 3072
SEQ = 512
SEGS = 4
ROWS = 64


def block_levels(stream_key, dims, shards, low, top_value):
    factor_of, own = 1.0, jax.random.fold_in(stream_key, 6)
    for dim, shards_of in shards:
        draws = jnp.exp(jax.random.uniform(jax.random.fold_in(own, dim), (shards_of,), jnp.float32, low / len(shards), top_value / len(shards)))
        factor_of = factor_of * jnp.repeat(draws, dims[dim] // shards_of).reshape([-1 if axis == dim else 1 for axis in range(len(dims))])
    return factor_of


def split_up(amount, total, reach, lean):
    weights = [(1 << 20) // math.isqrt(standing ** lean) + 1 for standing in range(2, amount + 1)]
    surplus, given = total - reach - (amount - 1), [1] * (amount - 1)
    while surplus > 0:
        movable = [i for i in range(amount - 1) if given[i] < reach]
        pool, left = sum([weights[i] for i in movable]), surplus
        for i in movable:
            more = min(reach - given[i], max(1, left * weights[i] // pool), surplus)
            given[i] = given[i] + more
            surplus = surplus - more
    return np.array([reach] + given)


def uneven_parts(own_key, number_of, total, reach, lean):
    if number_of == 2:
        one = jax.random.randint(own_key, (), max(1, total - reach), min(reach, total - 1) + 1)
        return jnp.stack([one, total - one])
    sizes = jnp.asarray(split_up(number_of, total, reach, lean), jnp.int32)
    couples = (number_of - 1) // 2
    giver, receiver = sizes[1:1 + 2 * couples:2], sizes[2:2 + 2 * couples:2]
    slack = jnp.minimum(giver - 1, reach - receiver)
    moved = jax.random.randint(jax.random.fold_in(own_key, 1), (couples,), 0, 1 << 20) % (slack + 1)
    sizes = sizes.at[1:1 + 2 * couples:2].set(giver - moved).at[2:2 + 2 * couples:2].set(receiver + moved)
    return sizes[jax.random.permutation(jax.random.fold_in(own_key, 2), number_of)]


def normal_values(key, shape, scale, most, cuts=(), kind=jnp.bfloat16):
    loudness = block_levels(key, shape, cuts, -0.22, 0.18) if cuts else 1.0
    array = jax.random.normal(key, shape, jnp.float32) * scale * loudness
    return jnp.minimum(jnp.maximum(array, -most), most).astype(kind)


def setup_inputs(seed: int = 0) -> dict:
    splits = jax.random.split(jax.random.key(seed), 19)
    return {
        "inputs": normal_values(splits[0], (ROWS, SEQ, D), 1.0, 6.0, ((0, 32),)),
        "segments": jax.vmap(lambda own: jnp.searchsorted(jnp.cumsum(uneven_parts(own, SEGS, SEQ, SEQ // 2, 2)), jnp.arange(SEQ), side="right"))(jax.random.split(splits[1], ROWS)).reshape((ROWS, SEQ)).astype(jnp.int32),
        "query_weight": normal_values(splits[2], (D * D,), D ** -0.5, 0.21875, ((0, 32),)),
        "query_bias": normal_values(splits[3], (D,), 0.5, 3.0, ((0, 32),)),
        "key_weight": normal_values(splits[4], (D * D,), D ** -0.5, 0.21875, ((0, 32),)),
        "value_weight": normal_values(splits[5], (D * D,), D ** -0.5, 0.21875, ((0, 32),)),
        "value_bias": normal_values(splits[6], (D,), 0.5, 3.0, ((0, 32),)),
        "output_weight": normal_values(splits[7], (D * D,), (D // 8) ** -0.5, 0.625, ((0, 32),)),
        "output_bias": normal_values(splits[8], (D,), 0.3, 2.0, ((0, 32),)),
        "attn_gain": jnp.clip(1.0 + 0.1 * jax.random.normal(splits[9], (D,), jnp.float32), 0.5, 1.5).astype(jnp.bfloat16),
        "attn_shift": normal_values(splits[10], (D,), 0.3, 2.0, ((0, 32),)),
        "inner_weight": normal_values(splits[11], (D * FF,), D ** -0.5, 0.21875, ((0, 32),)),
        "inner_bias": normal_values(splits[12], (FF,), 0.5, 3.0, ((0, 32),)),
        "outer_weight": normal_values(splits[13], (FF * D,), FF ** -0.5, 0.109375, ((0, 32),)),
        "outer_bias": normal_values(splits[14], (D,), 0.3, 2.0, ((0, 32),)),
        "ffn_gain": jnp.clip(1.0 + 0.1 * jax.random.normal(splits[15], (D,), jnp.float32), 0.5, 1.5).astype(jnp.bfloat16),
        "ffn_shift": normal_values(splits[16], (D,), 0.3, 2.0, ((0, 32),)),
        "cotangent": normal_values(splits[17], (ROWS, SEQ, D), 1.0, 6.0, ((0, 32),)),
    }


@jax.custom_vjp
def low(v):
    return lax.optimization_barrier(v.astype(jnp.bfloat16)).astype(jnp.float32)

@jax.custom_vjp
def low_back(v):
    return v

def low_keep(v):
    return (low(v), None)

def low_pass(kept, grad):
    return (grad,)

def back_keep(v):
    return (v, None)

def back_low(kept, grad):
    return (low(grad),)
low.defvjp(low_keep, low_pass)
low_back.defvjp(back_keep, back_low)
epsilon = 1e-06
masked_score = -1e+30

def rounded_both(value):
    return low(low_back(value))

def matmul(left, right):
    return jnp.dot(left, right, precision=lax.Precision.HIGHEST, preferred_element_type=jnp.float32)

def layer_norm(hidden, gain, shift):
    average = lax.optimization_barrier(jnp.mean(hidden, axis=-1, keepdims=True))
    centered = hidden - average
    variance = lax.optimization_barrier(jnp.mean(centered * centered, axis=-1, keepdims=True))
    return centered * lax.rsqrt(variance + epsilon) * gain + shift

def forward(params, inputs, segments):
    w_query, b_query, w_key, w_value, b_value, w_out, b_out, gain_one, shift_one, w_inner, b_inner, w_outer, b_outer, gain_two, shift_two = params
    group, length, width = inputs.shape
    flat = low(inputs.reshape(group * length, width))
    query = rounded_both(matmul(flat, low(w_query.reshape(D, D))) + b_query)
    key_rows = rounded_both(matmul(flat, low(w_key.reshape(D, D))))
    value_rows = rounded_both(matmul(flat, low(w_value.reshape(D, D))) + b_value)
    query_heads = query.reshape(group, length, H, HD)
    key_heads = key_rows.reshape(group, length, H, HD)
    value_heads = value_rows.reshape(group, length, H, HD)
    scores = jnp.einsum('rqhe,rkhe->rhqk', query_heads, key_heads, precision=lax.Precision.HIGHEST)
    scores = low_back(scores * HD ** (-0.5))
    same = segments[:, :, None] == segments[:, None, :]
    scores = jnp.where(same[:, None], scores, masked_score)
    top = lax.optimization_barrier(jnp.max(scores, axis=-1, keepdims=True))
    exponent = jnp.exp(scores - top)
    attention = low(exponent / lax.optimization_barrier(jnp.sum(exponent, axis=-1, keepdims=True)))
    context = jnp.einsum('rhqk,rkhe->rqhe', attention, value_heads, precision=lax.Precision.HIGHEST)
    context = rounded_both(context.reshape(group * length, D))
    attended = low_back(matmul(context, low(w_out.reshape(D, D))) + b_out)
    first = layer_norm(flat + attended, gain_one, shift_one)
    inner = low_back(matmul(low(first), low(w_inner.reshape(D, FF))) + b_inner)
    active = low(0.5 * inner * (1.0 + lax.erf(inner * 0.7071067811865476)))
    outer = low_back(matmul(active, low(w_outer.reshape(FF, D))) + b_outer)
    result = layer_norm(first + outer, gain_two, shift_two)
    return result.reshape(group, length, width)

def reference(inputs, segments, query_weight, query_bias, key_weight, value_weight, value_bias, output_weight, output_bias, attn_gain, attn_shift, inner_weight, inner_bias, outer_weight, outer_bias, ffn_gain, ffn_shift, cotangent):
    params = tuple((item.astype(jnp.float32) for item in (query_weight, query_bias, key_weight, value_weight, value_bias, output_weight, output_bias, attn_gain, attn_shift, inner_weight, inner_bias, outer_weight, outer_bias, ffn_gain, ffn_shift)))
    group = math.gcd(ROWS, max(1, 4096 // SEQ))
    steps_count = ROWS // group
    rows_in = inputs.astype(jnp.float32).reshape(steps_count, group, SEQ, D)
    rows_seg = segments.astype(jnp.int32).reshape(steps_count, group, SEQ)
    rows_cot = cotangent.astype(jnp.float32).reshape(steps_count, group, SEQ, D)

    def one_group(totals, pieces):
        block_in, block_seg, block_cot = pieces

        def apply_layer(layer_params, layer_in):
            return forward(layer_params, layer_in, block_seg)
        result, pull = jax.vjp(apply_layer, params, block_in)
        grad_params, grad_in = pull(block_cot)
        totals = tuple((left + right for left, right in zip(totals, grad_params)))
        return (totals, (result.astype(jnp.bfloat16), grad_in.astype(jnp.bfloat16)))
    zeros = tuple((jnp.zeros(item.shape, jnp.float32) for item in params))
    totals, (results, grads_in) = lax.scan(one_group, zeros, (rows_in, rows_seg, rows_cot))
    return (results.reshape(ROWS, SEQ, D), grads_in.reshape(ROWS, SEQ, D), totals[0], totals[1], totals[2], totals[3], totals[4], totals[5], totals[6], totals[7], totals[8], totals[9], totals[10], totals[11], totals[12], totals[13], totals[14])
```

```python
import jax
import jax.numpy as jnp
from jax import lax
from jax.sharding import PartitionSpec as P

D = 768
H = 12
HD = 64
FF = 3072


epsilon = 1e-06
masked_score = -1e30
root_half = 0.7071067811865476
inverse_root_twopi = 0.3989422804014327


def matmul(left, right):
    return jnp.dot(left, right, preferred_element_type=jnp.float32)


def matmul_left_t(left, right):
    return lax.dot_general(
        left, right, (((0,), (0,)), ((), ())), preferred_element_type=jnp.float32
    )


def matmul_right_t(left, right):
    return lax.dot_general(
        left, right, (((1,), (1,)), ((), ())), preferred_element_type=jnp.float32
    )


def norm_forward(hidden, gain, shift):
    average = jnp.mean(hidden, axis=-1, keepdims=True)
    centered = hidden - average
    variance = jnp.mean(centered * centered, axis=-1, keepdims=True)
    inv_std = lax.rsqrt(variance + epsilon)
    normed = centered * inv_std
    return (normed * gain + shift, normed, inv_std)


def norm_backward(upstream, normed, inv_std, gain):
    gain_grad = jnp.sum(upstream * normed, axis=0)
    shift_grad = jnp.sum(upstream, axis=0)
    scaled = upstream * gain
    scaled_mean = jnp.mean(scaled, axis=-1, keepdims=True)
    cross_mean = jnp.mean(scaled * normed, axis=-1, keepdims=True)
    return (inv_std * (scaled - scaled_mean - normed * cross_mean), gain_grad, shift_grad)


def gelu_value(inner):
    return 0.5 * inner * (1.0 + lax.erf(inner * root_half))


def gelu_slope(inner):
    return (
        0.5 * (1.0 + lax.erf(inner * root_half))
        + inner * jnp.exp(-0.5 * inner * inner) * inverse_root_twopi
    )


def split_heads(block):
    return block.reshape(block.shape[0], H, HD)


def row_scores(query, key_rows, segment):
    scores = jnp.einsum(
        "qhe,khe->hqk",
        split_heads(query),
        split_heads(key_rows),
        preferred_element_type=jnp.float32,
    ) * HD ** (-0.5)
    same = segment[:, None] == segment[None, :]
    return jnp.where(same[None], scores, masked_score)


def attend_forward(pieces):
    query, key_rows, value_rows, segment = pieces
    scores = row_scores(query, key_rows, segment)
    top = jnp.max(scores, axis=-1, keepdims=True)
    exponent = jnp.exp(scores - top)
    total = jnp.sum(exponent, axis=-1, keepdims=True)
    attention = (exponent / total).astype(jnp.bfloat16)
    context = jnp.einsum(
        "hqk,khe->qhe", attention, split_heads(value_rows), preferred_element_type=jnp.float32
    )
    return (context.reshape(query.shape).astype(jnp.bfloat16), (top + jnp.log(total))[..., 0])


def attend_backward(pieces):
    query, key_rows, value_rows, segment, logsum, context_grad = pieces
    scores = row_scores(query, key_rows, segment)
    attention = jnp.exp(scores - logsum[..., None])
    attention_low = attention.astype(jnp.bfloat16)
    grad_heads = split_heads(context_grad)
    value_grad = jnp.einsum(
        "hqk,qhe->khe", attention_low, grad_heads, preferred_element_type=jnp.float32
    )
    attention_grad = jnp.einsum(
        "qhe,khe->hqk", grad_heads, split_heads(value_rows), preferred_element_type=jnp.float32
    )
    inner_sum = jnp.sum(attention * attention_grad, axis=-1, keepdims=True)
    score_grad = (attention * (attention_grad - inner_sum)).astype(jnp.bfloat16)
    query_grad = jnp.einsum(
        "hqk,khe->qhe", score_grad, split_heads(key_rows), preferred_element_type=jnp.float32
    ) * HD ** (-0.5)
    key_grad = jnp.einsum(
        "hqk,qhe->khe", score_grad, split_heads(query), preferred_element_type=jnp.float32
    ) * HD ** (-0.5)
    shape = query.shape
    return (
        query_grad.reshape(shape).astype(jnp.bfloat16),
        key_grad.reshape(shape).astype(jnp.bfloat16),
        value_grad.reshape(shape).astype(jnp.bfloat16),
    )


def per_device(
    inputs,
    segments,
    query_weight,
    query_bias,
    key_weight,
    value_weight,
    value_bias,
    output_weight,
    output_bias,
    attn_gain,
    attn_shift,
    inner_weight,
    inner_bias,
    outer_weight,
    outer_bias,
    ffn_gain,
    ffn_shift,
    cotangent,
):
    rows, length, width = inputs.shape
    count = rows * length
    piece = query_bias.shape[0]
    devices = D // piece
    share = FF // D
    small = jnp.concatenate(
        (
            query_bias,
            value_bias,
            output_bias,
            attn_gain,
            attn_shift,
            outer_bias,
            ffn_gain,
            ffn_shift,
            inner_bias,
        )
    )
    small_rows = jnp.pad(small.reshape(1, -1), ((0, 7), (0, D - small.shape[0])))
    head = jnp.concatenate(
        (
            query_weight.reshape(piece, D),
            key_weight.reshape(piece, D),
            value_weight.reshape(piece, D),
            small_rows,
        )
    )
    inner_local = inner_weight.reshape(piece, FF)
    tail = jnp.concatenate(
        (
            output_weight.reshape(piece, D),
            outer_weight.reshape(share * piece, D),
            inner_local[:, 0:D],
            inner_local[:, D : 2 * D],
            inner_local[:, 2 * D : 3 * D],
            inner_local[:, 3 * D :],
        )
    )
    head_full = lax.all_gather(head, "fsdp", axis=0, tiled=True).reshape(devices, -1, D)
    tail_full = lax.all_gather(tail, "fsdp", axis=0, tiled=True).reshape(devices, -1, D)

    def weight(full, start, size):
        return full[:, start : start + size].reshape(devices * size, D)

    w_query = weight(head_full, 0, piece)
    w_key = weight(head_full, piece, piece)
    w_value = weight(head_full, 2 * piece, piece)
    w_output = weight(tail_full, 0, piece)
    w_outer = weight(tail_full, piece, share * piece)
    w_inner = jnp.concatenate(
        [weight(tail_full, (1 + share + i) * piece, piece) for i in range(share)], axis=1
    )
    small_full = head_full[:, 3 * piece, : (8 + share) * piece].astype(jnp.float32)
    vectors = small_full[:, : 8 * piece].reshape(devices, 8, piece).transpose(1, 0, 2).reshape(8, D)
    b_query, b_value, b_output, gain_one, shift_one, b_outer, gain_two, shift_two = (
        vectors[i] for i in range(8)
    )
    b_inner = small_full[:, 8 * piece :].reshape(FF)

    def shaped(block):
        return block.reshape(rows, length, D)

    flat = inputs.reshape(count, D)
    query = (matmul(flat, w_query) + b_query).astype(jnp.bfloat16)
    key_rows = matmul(flat, w_key).astype(jnp.bfloat16)
    value_rows = (matmul(flat, w_value) + b_value).astype(jnp.bfloat16)
    context, logsum = lax.map(
        attend_forward, (shaped(query), shaped(key_rows), shaped(value_rows), segments)
    )
    context = context.reshape(count, D)
    attended = matmul(context, w_output) + b_output
    first, normed_one, inv_one = norm_forward(
        flat.astype(jnp.float32) + attended, gain_one, shift_one
    )
    first_low = first.astype(jnp.bfloat16)
    inner = matmul(first_low, w_inner) + b_inner
    active = gelu_value(inner).astype(jnp.bfloat16)
    outer = matmul(active, w_outer) + b_outer
    result, normed_two, inv_two = norm_forward(first + outer, gain_two, shift_two)
    upstream = cotangent.reshape(count, D).astype(jnp.float32)
    second_grad, ffn_gain_grad, ffn_shift_grad = norm_backward(
        upstream, normed_two, inv_two, gain_two
    )
    outer_grad = second_grad.astype(jnp.bfloat16)
    outer_bias_grad = jnp.sum(outer_grad.astype(jnp.float32), axis=0)
    outer_weight_grad = matmul_left_t(active, outer_grad)
    inner_grad = (matmul_right_t(outer_grad, w_outer) * gelu_slope(inner)).astype(jnp.bfloat16)
    inner_bias_grad = jnp.sum(inner_grad.astype(jnp.float32), axis=0)
    inner_weight_grads = [
        matmul_left_t(first_low, inner_grad[:, i * D : (i + 1) * D]) for i in range(share)
    ]

    def terms(grad):
        return grad.astype(jnp.bfloat16).reshape(devices, -1, D)

    ffn_terms = jnp.concatenate(
        [terms(outer_weight_grad)] + [terms(block) for block in inner_weight_grads], axis=1
    )
    ffn_sum = lax.psum_scatter(
        ffn_terms.reshape(-1, D), "fsdp", scatter_dimension=0, tiled=True
    ).astype(jnp.float32)
    first_grad = second_grad + matmul_right_t(inner_grad, w_inner)
    attn_pre_grad, attn_gain_grad, attn_shift_grad = norm_backward(
        first_grad, normed_one, inv_one, gain_one
    )
    attended_grad = attn_pre_grad.astype(jnp.bfloat16)
    output_bias_grad = jnp.sum(attended_grad.astype(jnp.float32), axis=0)
    output_weight_grad = matmul_left_t(context, attended_grad)
    context_grad = matmul_right_t(attended_grad, w_output).astype(jnp.bfloat16)
    query_grad, key_grad, value_grad = lax.map(
        attend_backward,
        (
            shaped(query),
            shaped(key_rows),
            shaped(value_rows),
            segments,
            logsum,
            shaped(context_grad),
        ),
    )
    query_grad = query_grad.reshape(count, D)
    key_grad = key_grad.reshape(count, D)
    value_grad = value_grad.reshape(count, D)
    query_weight_grad = matmul_left_t(flat, query_grad)
    key_weight_grad = matmul_left_t(flat, key_grad)
    value_weight_grad = matmul_left_t(flat, value_grad)
    query_bias_grad = jnp.sum(query_grad.astype(jnp.float32), axis=0)
    value_bias_grad = jnp.sum(value_grad.astype(jnp.float32), axis=0)
    small_terms = jnp.stack(
        (
            query_bias_grad,
            value_bias_grad,
            output_bias_grad,
            attn_gain_grad,
            attn_shift_grad,
            outer_bias_grad,
            ffn_gain_grad,
            ffn_shift_grad,
        )
    )
    small_terms = jnp.concatenate(
        (
            small_terms.reshape(8, devices, piece).transpose(1, 0, 2).reshape(devices, 8 * piece),
            inner_bias_grad.reshape(devices, share * piece),
        ),
        axis=1,
    ).astype(jnp.bfloat16)
    small_terms = jnp.pad(
        small_terms[:, None, :], ((0, 0), (0, 7), (0, D - small_terms.shape[1]))
    )
    attn_terms = jnp.concatenate(
        (
            terms(output_weight_grad),
            terms(query_weight_grad),
            terms(key_weight_grad),
            terms(value_weight_grad),
            small_terms,
        ),
        axis=1,
    )
    attn_sum = lax.psum_scatter(
        attn_terms.reshape(-1, D), "fsdp", scatter_dimension=0, tiled=True
    ).astype(jnp.float32)
    input_grad = (
        attn_pre_grad
        + matmul_right_t(query_grad, w_query)
        + matmul_right_t(key_grad, w_key)
        + matmul_right_t(value_grad, w_value)
    )

    def owned(total, start, size):
        return total[start : start + size].reshape(-1)

    small_sum = attn_sum[4 * piece, : (8 + share) * piece]

    def vector(i, size=1):
        return small_sum[i * piece : (i + size) * piece]

    inner_sum = jnp.concatenate(
        [ffn_sum[(share + i) * piece : (share + i + 1) * piece] for i in range(share)], axis=1
    )
    return (
        result.reshape(rows, length, D).astype(jnp.bfloat16),
        input_grad.reshape(rows, length, D).astype(jnp.bfloat16),
        owned(attn_sum, piece, piece),
        vector(0),
        owned(attn_sum, 2 * piece, piece),
        owned(attn_sum, 3 * piece, piece),
        vector(1),
        owned(attn_sum, 0, piece),
        vector(2),
        vector(3),
        vector(4),
        inner_sum.reshape(-1),
        vector(8, share),
        owned(ffn_sum, 0, share * piece),
        vector(5),
        vector(6),
        vector(7),
    )


def solution(mesh):
    return jax.shard_map(
        per_device,
        mesh=mesh,
        in_specs=(
            P("fsdp", None, None),
            P("fsdp", None),
            P("fsdp"),
            P("fsdp"),
            P("fsdp"),
            P("fsdp"),
            P("fsdp"),
            P("fsdp"),
            P("fsdp"),
            P("fsdp"),
            P("fsdp"),
            P("fsdp"),
            P("fsdp"),
            P("fsdp"),
            P("fsdp"),
            P("fsdp"),
            P("fsdp"),
            P("fsdp", None, None),
        ),
        out_specs=(
            P("fsdp", None, None),
            P("fsdp", None, None),
            P("fsdp"),
            P("fsdp"),
            P("fsdp"),
            P("fsdp"),
            P("fsdp"),
            P("fsdp"),
            P("fsdp"),
            P("fsdp"),
            P("fsdp"),
            P("fsdp"),
            P("fsdp"),
            P("fsdp"),
            P("fsdp"),
            P("fsdp"),
            P("fsdp"),
        ),
        check_vma=False,
    )
```

```python
import jax
import jax.numpy as jnp
from jax import lax
from jax.experimental import pallas as pl
from jax.experimental.pallas import tpu as pltpu
from jax.sharding import PartitionSpec as P

D = 768
H = 12
HD = 64
FF = 3072


epsilon = 1e-06
masked_score = -1e30
root_half = 0.7071067811865476
inverse_root_twopi = 0.3989422804014327


def matmul(left, right):
    return jnp.dot(left, right, preferred_element_type=jnp.float32)


def matmul_left_t(left, right):
    return lax.dot_general(
        left, right, (((0,), (0,)), ((), ())), preferred_element_type=jnp.float32
    )


def matmul_right_t(left, right):
    return lax.dot_general(
        left, right, (((1,), (1,)), ((), ())), preferred_element_type=jnp.float32
    )


def norm_forward(hidden, gain, shift):
    average = jnp.mean(hidden, axis=-1, keepdims=True)
    centered = hidden - average
    variance = jnp.mean(centered * centered, axis=-1, keepdims=True)
    inv_std = lax.rsqrt(variance + epsilon)
    normed = centered * inv_std
    return (normed * gain + shift, normed, inv_std)


def norm_backward(upstream, normed, inv_std, gain):
    gain_grad = jnp.sum(upstream * normed, axis=0)
    shift_grad = jnp.sum(upstream, axis=0)
    scaled = upstream * gain
    scaled_mean = jnp.mean(scaled, axis=-1, keepdims=True)
    cross_mean = jnp.mean(scaled * normed, axis=-1, keepdims=True)
    return (inv_std * (scaled - scaled_mean - normed * cross_mean), gain_grad, shift_grad)


def gelu_value(inner):
    return 0.5 * inner * (1.0 + lax.erf(inner * root_half))


def gelu_slope(inner):
    return (
        0.5 * (1.0 + lax.erf(inner * root_half))
        + inner * jnp.exp(-0.5 * inner * inner) * inverse_root_twopi
    )


def contract(left, right, left_axis, right_axis):
    return lax.dot_general(
        left, right, (((left_axis,), (right_axis,)), ((), ())), preferred_element_type=jnp.float32
    )


def own_lanes(block, half):
    lane = lax.broadcasted_iota(jnp.int32, block.shape, 1)
    return jnp.where((lane >= HD) == bool(half), block, jnp.zeros_like(block))


def fill_mask(pair, column_ref, row_ref, mask_ref):
    @pl.when(pair == 0)
    def _():
        same = column_ref[...] == row_ref[...]
        mask_ref[...] = jnp.where(same, 0.0, masked_score)


def forward_kernel(query_ref, key_ref, value_ref, column_ref, row_ref, out_ref, log_ref, mask_ref):
    fill_mask(pl.program_id(1), column_ref, row_ref, mask_ref)
    key_rows, value_rows = key_ref[...], value_ref[...]
    scaled = query_ref[...] * jnp.bfloat16(HD ** (-0.5))
    halves = []
    for half in range(2):
        scores = contract(key_rows, own_lanes(scaled, half), 1, 1) + mask_ref[...]
        top = jnp.max(scores, axis=0, keepdims=True)
        exponent = jnp.exp(scores - top)
        total = jnp.sum(exponent, axis=0, keepdims=True)
        attention = (exponent * (1.0 / total)).astype(jnp.bfloat16)
        halves.append(contract(value_rows, attention, 0, 0)[half * HD : (half + 1) * HD])
        log_ref[half : half + 1, :] = top + jnp.log(total)
    out_ref[...] = jnp.concatenate(halves, axis=0).T.astype(jnp.bfloat16)


def backward_kernel(
    query_ref,
    key_ref,
    value_ref,
    grad_ref,
    column_ref,
    row_ref,
    log_ref,
    query_out,
    key_out,
    value_out,
    mask_ref,
):
    fill_mask(pl.program_id(1), column_ref, row_ref, mask_ref)
    key_rows, value_rows, grad = key_ref[...], value_ref[...], grad_ref[...]
    scaled = query_ref[...] * jnp.bfloat16(HD ** (-0.5))
    query_halves, key_total, value_total = [], None, None
    for half in range(2):
        scaled_own, grad_own = own_lanes(scaled, half), own_lanes(grad, half)
        scores = contract(key_rows, scaled_own, 1, 1) + mask_ref[...]
        attention = jnp.exp(scores - log_ref[half : half + 1, :])
        value_grad = contract(attention.astype(jnp.bfloat16), grad_own, 1, 0)
        attention_grad = contract(value_rows, grad_own, 1, 1)
        inner_sum = jnp.sum(attention * attention_grad, axis=0, keepdims=True)
        score_grad = (attention * (attention_grad - inner_sum)).astype(jnp.bfloat16)
        key_grad = contract(score_grad, scaled_own, 1, 0)
        query_halves.append(contract(key_rows, score_grad, 0, 0)[half * HD : (half + 1) * HD])
        key_total = key_grad if half == 0 else key_total + key_grad
        value_total = value_grad if half == 0 else value_total + value_grad
    query_grad = jnp.concatenate(query_halves, axis=0) * HD ** (-0.5)
    query_out[...] = query_grad.T.astype(jnp.bfloat16)
    key_out[...] = key_total.astype(jnp.bfloat16)
    value_out[...] = value_total.astype(jnp.bfloat16)


def attention_specs(rows, length):
    pairs = H // 2
    block = pl.BlockSpec((length, 2 * HD), lambda r, p: (r, p))
    column = pl.BlockSpec((None, length, 1), lambda r, p: (r, 0, 0))
    row = pl.BlockSpec((None, 1, length), lambda r, p: (r, 0, 0))
    logs = pl.BlockSpec((None, None, 2, length), lambda r, p: (r, p, 0, 0))
    options = dict(
        grid=(rows, pairs),
        scratch_shapes=[pltpu.VMEM((length, length), jnp.float32)],
        compiler_params=pltpu.CompilerParams(dimension_semantics=("arbitrary", "arbitrary")),
    )
    return block, column, row, logs, options


def attend_forward(query, key_rows, value_rows, segments):
    rows, length = segments.shape
    block, column, row, logs, options = attention_specs(rows, length)
    return pl.pallas_call(
        forward_kernel,
        name="attend_forward",
        in_specs=[block, block, block, column, row],
        out_specs=[block, logs],
        out_shape=[
            jax.ShapeDtypeStruct(query.shape, jnp.bfloat16),
            jax.ShapeDtypeStruct((rows, H // 2, 2, length), jnp.float32),
        ],
        cost_estimate=pl.CostEstimate(
            flops=8 * rows * H * length * length * HD,
            bytes_accessed=8 * rows * length * D,
            transcendentals=rows * H * length * length,
        ),
        **options,
    )(query, key_rows, value_rows, segments[:, :, None], segments[:, None, :])


def attend_backward(query, key_rows, value_rows, grad, segments, logsum):
    rows, length = segments.shape
    block, column, row, logs, options = attention_specs(rows, length)
    return pl.pallas_call(
        backward_kernel,
        name="attend_backward",
        in_specs=[block, block, block, block, column, row, logs],
        out_specs=[block, block, block],
        out_shape=[jax.ShapeDtypeStruct(query.shape, jnp.bfloat16)] * 3,
        cost_estimate=pl.CostEstimate(
            flops=20 * rows * H * length * length * HD,
            bytes_accessed=14 * rows * length * D,
            transcendentals=rows * H * length * length,
        ),
        **options,
    )(query, key_rows, value_rows, grad, segments[:, :, None], segments[:, None, :], logsum)


def partners(devices, bit):
    return [(i, i ^ (1 << bit)) for i in range(devices)]


def gather_blocks(block, devices):
    me = lax.axis_index("fsdp")
    held = block[None]
    for bit in reversed(range(devices.bit_length() - 1)):
        other = lax.ppermute(held, "fsdp", partners(devices, bit))
        upper = ((me >> bit) & 1) == 1
        held = jnp.stack(
            (jnp.where(upper, other, held), jnp.where(upper, held, other)), axis=1
        ).reshape((-1,) + block.shape)
    return held


def scatter_blocks(terms, devices):
    me = lax.axis_index("fsdp")
    for bit in range(devices.bit_length() - 1):
        pairs = terms.reshape((-1, 2) + terms.shape[1:])
        upper = ((me >> bit) & 1) == 1
        keep = jnp.where(upper, pairs[:, 1], pairs[:, 0])
        send = jnp.where(upper, pairs[:, 0], pairs[:, 1])
        other = lax.ppermute(send, "fsdp", partners(devices, bit))
        terms = (keep.astype(jnp.float32) + other.astype(jnp.float32)).astype(jnp.bfloat16)
    return terms[0]


def per_device(
    inputs,
    segments,
    query_weight,
    query_bias,
    key_weight,
    value_weight,
    value_bias,
    output_weight,
    output_bias,
    attn_gain,
    attn_shift,
    inner_weight,
    inner_bias,
    outer_weight,
    outer_bias,
    ffn_gain,
    ffn_shift,
    cotangent,
):
    rows, length, width = inputs.shape
    count = rows * length
    piece = query_bias.shape[0]
    devices = D // piece
    share = FF // D
    small = jnp.concatenate(
        (
            query_bias,
            value_bias,
            output_bias,
            attn_gain,
            attn_shift,
            outer_bias,
            ffn_gain,
            ffn_shift,
            inner_bias,
        )
    )
    small_rows = jnp.pad(small.reshape(1, -1), ((0, 7), (0, D - small.shape[0])))
    head = jnp.concatenate(
        (
            query_weight.reshape(piece, D),
            key_weight.reshape(piece, D),
            value_weight.reshape(piece, D),
            small_rows,
        )
    )
    inner_local = inner_weight.reshape(piece, FF)
    tail = jnp.concatenate(
        (
            output_weight.reshape(piece, D),
            outer_weight.reshape(share * piece, D),
            inner_local[:, 0:D],
            inner_local[:, D : 2 * D],
            inner_local[:, 2 * D : 3 * D],
            inner_local[:, 3 * D :],
        )
    )
    head_full = gather_blocks(head, devices)
    tail_full = lax.all_gather(tail, "fsdp", axis=0, tiled=True).reshape(devices, -1, D)

    def weight(full, start, size):
        return full[:, start : start + size].reshape(devices * size, D)

    w_query = weight(head_full, 0, piece)
    w_key = weight(head_full, piece, piece)
    w_value = weight(head_full, 2 * piece, piece)
    w_output = weight(tail_full, 0, piece)
    w_outer = weight(tail_full, piece, share * piece)
    w_inner = jnp.concatenate(
        [weight(tail_full, (1 + share + i) * piece, piece) for i in range(share)], axis=1
    )
    small_full = head_full[:, 3 * piece, : (8 + share) * piece].astype(jnp.float32)
    vectors = small_full[:, : 8 * piece].reshape(devices, 8, piece).transpose(1, 0, 2).reshape(8, D)
    b_query, b_value, b_output, gain_one, shift_one, b_outer, gain_two, shift_two = (
        vectors[i] for i in range(8)
    )
    b_inner = small_full[:, 8 * piece :].reshape(FF)

    flat = inputs.reshape(count, D)
    query = (matmul(flat, w_query) + b_query).astype(jnp.bfloat16)
    key_rows = matmul(flat, w_key).astype(jnp.bfloat16)
    value_rows = (matmul(flat, w_value) + b_value).astype(jnp.bfloat16)
    context, logsum = attend_forward(query, key_rows, value_rows, segments)
    attended = matmul(context, w_output) + b_output
    first, normed_one, inv_one = norm_forward(
        flat.astype(jnp.float32) + attended, gain_one, shift_one
    )
    first_low = first.astype(jnp.bfloat16)
    inner = matmul(first_low, w_inner) + b_inner
    active = gelu_value(inner).astype(jnp.bfloat16)
    outer = matmul(active, w_outer) + b_outer
    result, normed_two, inv_two = norm_forward(first + outer, gain_two, shift_two)
    upstream = cotangent.reshape(count, D).astype(jnp.float32)
    second_grad, ffn_gain_grad, ffn_shift_grad = norm_backward(
        upstream, normed_two, inv_two, gain_two
    )
    outer_grad = second_grad.astype(jnp.bfloat16)
    outer_bias_grad = jnp.sum(outer_grad.astype(jnp.float32), axis=0)
    outer_weight_grad = matmul_left_t(active, outer_grad)
    inner_grad = (matmul_right_t(outer_grad, w_outer) * gelu_slope(inner)).astype(jnp.bfloat16)
    inner_bias_grad = jnp.sum(inner_grad.astype(jnp.float32), axis=0)
    inner_weight_grads = [
        matmul_left_t(first_low, inner_grad[:, i * D : (i + 1) * D]) for i in range(share)
    ]

    def terms(grad):
        return grad.astype(jnp.bfloat16).reshape(devices, -1, D)

    first_grad = second_grad + matmul_right_t(inner_grad, w_inner)
    attn_pre_grad, attn_gain_grad, attn_shift_grad = norm_backward(
        first_grad, normed_one, inv_one, gain_one
    )
    attended_grad = attn_pre_grad.astype(jnp.bfloat16)
    output_bias_grad = jnp.sum(attended_grad.astype(jnp.float32), axis=0)
    output_weight_grad = matmul_left_t(context, attended_grad)
    context_grad = matmul_right_t(attended_grad, w_output).astype(jnp.bfloat16)
    early_terms = jnp.concatenate(
        [terms(outer_weight_grad)]
        + [terms(block) for block in inner_weight_grads]
        + [terms(output_weight_grad)],
        axis=1,
    ).reshape(-1, D)
    early_terms, context_grad = lax.optimization_barrier((early_terms, context_grad))
    ffn_sum = lax.psum_scatter(
        early_terms, "fsdp", scatter_dimension=0, tiled=True
    ).astype(jnp.float32)
    query_grad, key_grad, value_grad = attend_backward(
        query, key_rows, value_rows, context_grad, segments, logsum
    )
    query_weight_grad = matmul_left_t(flat, query_grad)
    key_weight_grad = matmul_left_t(flat, key_grad)
    value_weight_grad = matmul_left_t(flat, value_grad)
    query_bias_grad = jnp.sum(query_grad.astype(jnp.float32), axis=0)
    value_bias_grad = jnp.sum(value_grad.astype(jnp.float32), axis=0)
    small_terms = jnp.stack(
        (
            query_bias_grad,
            value_bias_grad,
            output_bias_grad,
            attn_gain_grad,
            attn_shift_grad,
            outer_bias_grad,
            ffn_gain_grad,
            ffn_shift_grad,
        )
    )
    small_terms = jnp.concatenate(
        (
            small_terms.reshape(8, devices, piece).transpose(1, 0, 2).reshape(devices, 8 * piece),
            inner_bias_grad.reshape(devices, share * piece),
        ),
        axis=1,
    ).astype(jnp.bfloat16)
    small_terms = jnp.pad(
        small_terms[:, None, :], ((0, 0), (0, 7), (0, D - small_terms.shape[1]))
    )
    attn_terms = jnp.concatenate(
        (
            terms(query_weight_grad),
            terms(key_weight_grad),
            terms(value_weight_grad),
            small_terms,
        ),
        axis=1,
    )
    attn_sum = scatter_blocks(attn_terms, devices).astype(jnp.float32)
    input_grad = (
        attn_pre_grad
        + matmul_right_t(query_grad, w_query)
        + matmul_right_t(key_grad, w_key)
        + matmul_right_t(value_grad, w_value)
    )

    def owned(total, start, size):
        return total[start : start + size].reshape(-1)

    small_sum = attn_sum[3 * piece, : (8 + share) * piece]

    def vector(i, size=1):
        return small_sum[i * piece : (i + size) * piece]

    inner_sum = jnp.concatenate(
        [ffn_sum[(share + i) * piece : (share + i + 1) * piece] for i in range(share)], axis=1
    )
    return (
        result.reshape(rows, length, D).astype(jnp.bfloat16),
        input_grad.reshape(rows, length, D).astype(jnp.bfloat16),
        owned(attn_sum, 0, piece),
        vector(0),
        owned(attn_sum, piece, piece),
        owned(attn_sum, 2 * piece, piece),
        vector(1),
        owned(ffn_sum, 2 * share * piece, piece),
        vector(2),
        vector(3),
        vector(4),
        inner_sum.reshape(-1),
        vector(8, share),
        owned(ffn_sum, 0, share * piece),
        vector(5),
        vector(6),
        vector(7),
    )


def solution(mesh):
    return jax.shard_map(
        per_device,
        mesh=mesh,
        in_specs=(
            P("fsdp", None, None),
            P("fsdp", None),
            P("fsdp"),
            P("fsdp"),
            P("fsdp"),
            P("fsdp"),
            P("fsdp"),
            P("fsdp"),
            P("fsdp"),
            P("fsdp"),
            P("fsdp"),
            P("fsdp"),
            P("fsdp"),
            P("fsdp"),
            P("fsdp"),
            P("fsdp"),
            P("fsdp"),
            P("fsdp", None, None),
        ),
        out_specs=(
            P("fsdp", None, None),
            P("fsdp", None, None),
            P("fsdp"),
            P("fsdp"),
            P("fsdp"),
            P("fsdp"),
            P("fsdp"),
            P("fsdp"),
            P("fsdp"),
            P("fsdp"),
            P("fsdp"),
            P("fsdp"),
            P("fsdp"),
            P("fsdp"),
            P("fsdp"),
            P("fsdp"),
            P("fsdp"),
        ),
        check_vma=False,
    )
```
